32 devices in a mesh: bx: 4 (over z), by: 8 (over y, x, core).
Axes of the slice: x: 2, y: 2, z: 4, core: 2. Of those that a mesh axis runs over, the one named last changes fastest.
Arguments:
- incident: float32 [2, 96, 4, 8, 128], P(None, None, 'bx', 'by'), may hold values from -6 to 6
- mie: float32 [2, 12, 4, 8, 128], P(None, None, 'bx', 'by'), may hold values from -1 to 1
- offsets: float32 [3, 4, 8, 128], P(None, 'bx', 'by'), may hold values from -1 to 1
- sphere_box: int32 [4, 8, 128], P('bx', 'by'), may hold values from 0 to 15
- near_table: bfloat16 [16, 2, 96, 96], replicated, may hold values from -0.078125 to 0.078125
- near_src: int32 [4, 8, 16, 256], P('bx', 'by'), may hold values from 0 to 1151
- near_dst: int32 [4, 8, 16, 256], P('bx', 'by'), may hold values from 0 to 127
- pattern: bfloat16 [2, 128, 96], replicated, may hold values from -0.84 to 0.84
- receive: bfloat16 [2, 96, 128], replicated, may hold values from -0.375 to 0.375
- leaf_transfer: float32 [32, 2, 128], replicated, may hold values from -0.15 to 0.15
- far_src: int32 [4, 8, 16, 24], P('bx', 'by'), may hold values from 0 to 143
- far_cls: int32 [4, 8, 16, 24], P('bx', 'by'), may hold values from 0 to 31
- coarse_transfer: float32 [2, 7, 15, 128], replicated, may hold values from -0.012 to 0.012
Outputs:
- solution: float32 [2, 96, 4, 8, 128], P(None, None, 'bx', 'by')
- residual: float32 [2, 96, 4, 8, 128], P(None, None, 'bx', 'by')
The draws below stay inside these ranges and needn't reach their ends.
All inputs are finite; a program needn't handle non-finite values.
Results may differ from the reference program's by a relative error of at most 0.0095.
Values may be sent and summed in bfloat16 or wider, within the bound.
A program may use at most 64 MiB of HBM per device.

```python
import math
import jax
import jax.numpy as jnp
import numpy as np
from jax import lax

NCOEF = 96
MIE = 12
DIRS = 128
SPH_DEV = 128
LEAF_BOX = 16
NEAR_CLS = 16
PAIRS = 256
LIST_LEN = 24
LEAF_CLS = 32
ITERS = 2
GRID_X = 4
GRID_Y = 8
N_BX = 4
N_BY = 8


DECAY_BASE = 0.6


MIE_TOP = 0.8


def order_gains(coef_count):
    half_count = coef_count // 2
    degrees = np.array([math.isqrt(number % half_count + 1) for number in range(coef_count)])
    raw_gain = DECAY_BASE ** (degrees - 1)
    scale_fix = math.sqrt(half_count / float(np.sum(raw_gain[:half_count] ** 2)))
    return (raw_gain * scale_fix).astype(np.float32)


def draw_mie(key, part):
    size_key = jax.random.fold_in(key, 11)
    angle_key = jax.random.fold_in(key, 12)
    shape = (MIE, GRID_X, GRID_Y, SPH_DEV)
    power = jax.random.uniform(size_key, shape, jnp.float32, 0.0, 1.0)
    factor = 0.5 * jnp.exp(power * math.log(2.5))
    factor = jnp.clip(factor, 0.5, 1.25)
    orders = np.arange(MIE) % (MIE // 2)
    decay = jnp.asarray((MIE_TOP * DECAY_BASE ** orders).astype(np.float32)).reshape(MIE, 1, 1, 1)
    angle = jax.random.uniform(angle_key, shape, jnp.float32, -math.pi, math.pi)
    magnitude = decay * factor
    return jnp.stack([magnitude * jnp.cos(angle), magnitude * jnp.sin(angle)]).astype(jnp.float32)


def draw_pattern(key, part):
    entry_key = jax.random.fold_in(key, 21)
    shape = (2, DIRS, NCOEF)
    values = jnp.clip(jax.random.normal(entry_key, shape, jnp.float32), -3.0, 3.0)
    gains = jnp.asarray(order_gains(NCOEF)).reshape(1, 1, NCOEF)
    return (values * gains / math.sqrt(NCOEF)).astype(jnp.bfloat16)


def set_ends(values, stream_key, least, high):
    longest = values.shape.index(max(values.shape))
    spots = []
    for shift in (0, 1):
        where = [jax.random.randint(jax.random.fold_in(stream_key, axis), (), 0, length) for axis, length in enumerate(values.shape)]
        where[longest] = (where[longest] + shift) % values.shape[longest]
        spots.append(tuple(where))
    return values.at[spots[0]].set(least).at[spots[1]].set(high)


def block_scale(key, shape, shards, least, high):
    gain = 1.0
    for position, shards_of in shards:
        steps = jax.random.uniform(jax.random.fold_in(jax.random.fold_in(key, 6), position), (shards_of,), jnp.float32, least / len(shards), high / len(shards))
        gain = gain * jnp.repeat(jnp.exp(steps), shape[position] // shards_of).reshape((-1,) + (1,) * (len(shape) - 1 - position))
    return gain


def noise(rng, shape, width, limit, pieces=(), held_as=jnp.bfloat16):
    values = jax.random.normal(rng, shape, jnp.float32) * width
    if len(pieces) > 0:
        values = block_scale(rng, shape, pieces, -0.22, 0.18) * values
    return jnp.clip(values, min=-limit, max=limit).astype(held_as)


def setup_inputs(seed: int = 0) -> dict:
    streams_of = jax.random.split(jax.random.key(seed), 14)
    incident = noise(streams_of[0], (2, NCOEF, GRID_X, GRID_Y, SPH_DEV), 1.0, 6.0, ((2, 4), (3, 8)), jnp.float32)
    mie = draw_mie(jax.random.fold_in(streams_of[13], 71), 0)
    offsets = jnp.clip(jax.random.uniform(streams_of[2], (3, GRID_X, GRID_Y, SPH_DEV), jnp.float32, -1.0, 1.0) * block_scale(streams_of[2], (3, GRID_X, GRID_Y, SPH_DEV), ((1, 4), (2, 8)), -0.4, 0.0), -1.0, 1.0)
    sphere_box = set_ends(jax.random.randint(streams_of[3], (GRID_X, GRID_Y, SPH_DEV), 0, LEAF_BOX), jax.random.fold_in(streams_of[3], 1), 0, LEAF_BOX - 1).astype(jnp.int32)
    near_table = noise(streams_of[4], (NEAR_CLS, 2, NCOEF, NCOEF), (2 * NCOEF * NEAR_CLS * PAIRS // SPH_DEV) ** -0.5, 0.078125)
    near_src = set_ends(jax.random.randint(streams_of[5], (GRID_X, GRID_Y, NEAR_CLS, PAIRS), 0, 9 * SPH_DEV), jax.random.fold_in(streams_of[5], 1), 0, (9 * SPH_DEV) - 1).astype(jnp.int32)
    near_dst = set_ends(jax.random.randint(streams_of[6], (GRID_X, GRID_Y, NEAR_CLS, PAIRS), 0, SPH_DEV), jax.random.fold_in(streams_of[6], 1), 0, SPH_DEV - 1).astype(jnp.int32)
    pattern = draw_pattern(jax.random.fold_in(streams_of[13], 71), 0)
    receive = noise(streams_of[8], (2, NCOEF, DIRS), (2 * DIRS) ** -0.5, 0.375)
    leaf_transfer = noise(streams_of[9], (LEAF_CLS, 2, DIRS), 0.025, 0.15, (), jnp.float32)
    far_src = set_ends(jax.random.randint(streams_of[10], (GRID_X, GRID_Y, LEAF_BOX, LIST_LEN), 0, 9 * LEAF_BOX), jax.random.fold_in(streams_of[10], 1), 0, (9 * LEAF_BOX) - 1).astype(jnp.int32)
    far_cls = set_ends(jax.random.randint(streams_of[11], (GRID_X, GRID_Y, LEAF_BOX, LIST_LEN), 0, LEAF_CLS), jax.random.fold_in(streams_of[11], 1), 0, LEAF_CLS - 1).astype(jnp.int32)
    coarse_transfer = noise(streams_of[12], (2, 2 * GRID_X - 1, 2 * GRID_Y - 1, DIRS), 0.002, 0.012, (), jnp.float32)
    return {"incident": incident, "mie": mie, "offsets": offsets, "sphere_box": sphere_box, "near_table": near_table, "near_src": near_src, "near_dst": near_dst, "pattern": pattern, "receive": receive, "leaf_transfer": leaf_transfer, "far_src": far_src, "far_cls": far_cls, "coarse_transfer": coarse_transfer}


HIGHEST = lax.Precision.HIGHEST
KAPPA = 1.5
GOLDEN = 2.399963229728653

def int_starts(values):
    return tuple((jnp.asarray(value).astype(jnp.int32) for value in values))

def directions(number):
    ordinal = jnp.arange(number).astype(jnp.float32)
    height = 1.0 - (2.0 * ordinal + 1.0) / number
    radius = jnp.sqrt(1.0 - height * height)
    return jnp.stack([radius * jnp.cos(GOLDEN * ordinal), radius * jnp.sin(GOLDEN * ordinal), height])

def leaf_centers(number):
    ordinal = jnp.arange(number, dtype=jnp.int32)
    first_c = 2.0 * (ordinal % 2).astype(jnp.float32) - 1.0
    second_c = 2.0 * (ordinal // 2 % 2).astype(jnp.float32) - 1.0
    third_c = 2.0 * (ordinal // 4).astype(jnp.float32) - (number // 4 - 1)
    return jnp.stack([first_c, second_c, third_c])

def mie_spread(coef_count, mie_count):
    half_count = coef_count // 2
    table = np.zeros((coef_count, mie_count), np.float32)
    for number in range(coef_count):
        within = number % half_count
        degree = math.isqrt(within + 1)
        table[number, number // half_count * (mie_count // 2) + degree - 1] = 1.0
    return table

def complex_block(matrix):
    real_part = matrix[..., 0, :, :]
    imag_part = matrix[..., 1, :, :]
    upper = jnp.concatenate([real_part, -imag_part], axis=-1)
    bottom = jnp.concatenate([imag_part, real_part], axis=-1)
    return jnp.concatenate([upper, bottom], axis=-2)

def rotate(real_part, imag_part, cosines, sine_vals):
    return (real_part * cosines - imag_part * sine_vals, real_part * sine_vals + imag_part * cosines)

def far_mask(first_pos, second_pos, across_x, across_y):
    ordinal = jnp.arange(across_x * across_y, dtype=jnp.int32)
    apart_x = jnp.abs(ordinal // across_y - first_pos)
    apart_y = jnp.abs(ordinal % across_y - second_pos)
    return ((apart_x >= 2) | (apart_y >= 2)).astype(jnp.float32)

def small_solve(normal, rhs_vec, size_count):
    lower_tri = jnp.linalg.cholesky(normal)
    middle = []
    for row_num in range(size_count):
        accum = rhs_vec[row_num]
        for col_num in range(row_num):
            accum = accum - lower_tri[row_num, col_num] * middle[col_num]
        middle.append(accum / lower_tri[row_num, row_num])
    weights = [None] * size_count
    for row_num in reversed(range(size_count)):
        accum = middle[row_num]
        for col_num in range(row_num + 1, size_count):
            accum = accum - lower_tri[col_num, row_num] * weights[col_num]
        weights[row_num] = accum / lower_tri[row_num, row_num]
    return weights

def reference(incident, mie, offsets, sphere_box, near_table, near_src, near_dst, pattern, receive, leaf_transfer, far_src, far_cls, coarse_transfer):
    total_cols = N_BX * N_BY
    block_rows = 2 * NCOEF
    flat_len = total_cols * SPH_DEV
    blocks = complex_block(near_table).astype(jnp.float32)
    send_block = complex_block(pattern)
    take_block = complex_block(receive)
    planes = directions(DIRS)
    phases = KAPPA * jnp.dot(planes.T, offsets.reshape(3, flat_len), precision=HIGHEST)
    cos_sphere, sin_sphere = (jnp.cos(phases), jnp.sin(phases))
    centre = KAPPA * jnp.dot(planes.T, leaf_centers(LEAF_BOX), precision=HIGHEST)
    cos_leaf, sin_leaf = (jnp.cos(centre), jnp.sin(centre))
    member = (sphere_box.reshape(total_cols, 1, SPH_DEV) == jnp.arange(LEAF_BOX, dtype=jnp.int32).reshape(1, LEAF_BOX, 1)).astype(jnp.float32)
    mie_full = jnp.einsum('nk,rks->rns', jnp.asarray(mie_spread(NCOEF, MIE)), mie.reshape(2, MIE, flat_len), precision=HIGHEST)
    cols_index = jnp.arange(total_cols, dtype=jnp.int32)

    def apply_operator(vector):
        rounded = vector.astype(jnp.bfloat16)
        padded = jnp.pad(rounded, ((0, 0), (0, 0), (1, 1), (1, 1), (0, 0)))

        def near_one(item):
            column, sources, targets = item
            first_pos, second_pos = (column // N_BY, column % N_BY)
            window = lax.dynamic_slice(padded, int_starts((0, 0, first_pos, second_pos, 0)), (2, NCOEF, 3, 3, SPH_DEV)).reshape(block_rows, 9 * SPH_DEV)
            picked = jnp.take(window, sources.reshape(-1), axis=1).reshape(block_rows, NEAR_CLS, PAIRS).astype(jnp.float32)
            contrib = jnp.einsum('kab,bkm->akm', blocks, picked, precision=HIGHEST)
            return jnp.zeros((block_rows, SPH_DEV), jnp.float32).at[:, targets.reshape(-1)].add(contrib.reshape(block_rows, NEAR_CLS * PAIRS))
        near = lax.map(near_one, (cols_index, near_src.reshape(total_cols, NEAR_CLS, PAIRS), near_dst.reshape(total_cols, NEAR_CLS, PAIRS)))
        near = near.transpose(1, 0, 2).reshape(block_rows, flat_len)
        signature = jnp.dot(send_block.astype(jnp.float32), rounded.reshape(block_rows, flat_len).astype(jnp.float32), preferred_element_type=jnp.float32)
        out_real, out_imag = rotate(signature[:DIRS], signature[DIRS:], cos_sphere, -sin_sphere)
        outgoing = jnp.concatenate([out_real, out_imag]).reshape(2 * DIRS, total_cols, SPH_DEV)
        leaf_out = jnp.einsum('rds,dbs->rdb', outgoing, member, precision=HIGHEST)
        leaf_pad = jnp.pad(leaf_out.reshape(2, DIRS, N_BX, N_BY, LEAF_BOX), ((0, 0), (0, 0), (1, 1), (1, 1), (0, 0)))

        def leaf_one(item):
            column, sources, classes = item
            first_pos, second_pos = (column // N_BY, column % N_BY)
            window = lax.dynamic_slice(leaf_pad, int_starts((0, 0, first_pos, second_pos, 0)), (2, DIRS, 3, 3, LEAF_BOX)).reshape(2, DIRS, 9 * LEAF_BOX)
            picked = jnp.take(window, sources.reshape(-1), axis=2)
            class_hot = (jnp.arange(LEAF_CLS, dtype=jnp.int32)[:, None] == classes.reshape(1, -1)).astype(jnp.float32)
            chosen = jnp.dot(leaf_transfer.reshape(LEAF_CLS, 2 * DIRS).T, class_hot, precision=HIGHEST).reshape(2, DIRS, LEAF_BOX * LIST_LEN)
            prod_real, prod_imag = rotate(picked[0], picked[1], chosen[0], chosen[1])
            return jnp.stack([prod_real, prod_imag]).reshape(2, DIRS, LEAF_BOX, LIST_LEN).sum(axis=3)
        leaf_in = lax.map(leaf_one, (cols_index, far_src.reshape(total_cols, LEAF_BOX, LIST_LEN), far_cls.reshape(total_cols, LEAF_BOX, LIST_LEN)))
        up_real, up_imag = rotate(leaf_out[:DIRS], leaf_out[DIRS:], cos_leaf[:, None, :], -sin_leaf[:, None, :])
        column_out = jnp.stack([up_real.sum(axis=2), up_imag.sum(axis=2)])

        def coarse_one(column):
            first_pos, second_pos = (column // N_BY, column % N_BY)
            window = lax.dynamic_slice(coarse_transfer, int_starts((0, N_BX - 1 - first_pos, N_BY - 1 - second_pos, 0)), (2, N_BX, N_BY, DIRS)).reshape(2, total_cols, DIRS)
            window = window.transpose(0, 2, 1) * far_mask(first_pos, second_pos, N_BX, N_BY)
            prod_real, prod_imag = rotate(column_out[0], column_out[1], window[0], window[1])
            return jnp.stack([prod_real.sum(axis=1), prod_imag.sum(axis=1)])
        column_in = lax.map(coarse_one, cols_index)
        down_real, down_imag = rotate(column_in[:, 0, :, None], column_in[:, 1, :, None], cos_leaf[None], sin_leaf[None])
        incoming = leaf_in + jnp.stack([down_real, down_imag], axis=1)
        spread = jnp.einsum('dxqb,dbs->xqds', incoming, member, precision=HIGHEST).reshape(2, DIRS, flat_len)
        in_real, in_imag = rotate(spread[0], spread[1], cos_sphere, sin_sphere)
        arriving = jnp.concatenate([in_real, in_imag]).astype(jnp.bfloat16)
        far = jnp.dot(take_block.astype(jnp.float32), arriving.astype(jnp.float32), preferred_element_type=jnp.float32)
        field_sum = near + far
        source = vector.reshape(2, NCOEF, flat_len)
        prod_real, prod_imag = rotate(field_sum[:NCOEF], field_sum[NCOEF:], mie_full[0], mie_full[1])
        return jnp.stack([source[0] - prod_real, source[1] - prod_imag]).reshape(vector.shape)
    beta_norm = jnp.sqrt(jnp.sum(incident * incident))
    basis_list = [incident / beta_norm]
    hess_mat = jnp.zeros((ITERS + 1, ITERS), jnp.float32)
    for col_num in range(ITERS):
        krylov_vec = apply_operator(basis_list[col_num])
        heights = [jnp.sum(krylov_vec * basis_item) for basis_item in basis_list]
        for row_num in range(col_num + 1):
            krylov_vec = krylov_vec - heights[row_num] * basis_list[row_num]
            hess_mat = hess_mat.at[row_num, col_num].set(heights[row_num])
        length = jnp.sqrt(jnp.sum(krylov_vec * krylov_vec))
        hess_mat = hess_mat.at[col_num + 1, col_num].set(length)
        basis_list.append(krylov_vec / length)
    normal = jnp.dot(hess_mat.T, hess_mat, precision=HIGHEST)
    weights = small_solve(normal, beta_norm * hess_mat[0], ITERS)
    solution = jnp.zeros_like(incident)
    for col_num in range(ITERS):
        solution = solution + weights[col_num] * basis_list[col_num]
    fitted = jnp.dot(hess_mat, jnp.stack(weights), precision=HIGHEST)
    residual = beta_norm * basis_list[0]
    for row_num in range(ITERS + 1):
        residual = residual - fitted[row_num] * basis_list[row_num]
    return (solution, residual)
```

```python
import functools
import math

import jax
import jax.numpy as jnp
import numpy as np
from jax import lax
from jax.experimental import pallas as pl
from jax.experimental.pallas import tpu as pltpu
from jax.sharding import PartitionSpec as P

KAPPA = 1.5
GOLDEN = 2.399963229728653
HIGHEST = lax.Precision.HIGHEST
F32 = jnp.float32
BF16 = jnp.bfloat16
MESH = pl.DeviceIdType.MESH
LANES = 128


def constants(dirs, boxes, coefs, mies):
    q = np.arange(dirs, dtype=np.float64)
    height = 1.0 - (2.0 * q + 1.0) / dirs
    radius = np.sqrt(1.0 - height * height)
    planes = np.stack([radius * np.cos(GOLDEN * q), radius * np.sin(GOLDEN * q), height], axis=1)
    b = np.arange(boxes)
    centers = np.stack([2.0 * (b % 2) - 1.0, 2.0 * (b // 2 % 2) - 1.0, 2.0 * (b // 4) - (boxes // 4 - 1)])
    centre = KAPPA * (planes @ centers)
    table = np.zeros((dirs + 2 * boxes, LANES), np.float64)
    table[:dirs, :3] = KAPPA * planes
    half = coefs // 2
    for n in range(coefs):
        degree = math.isqrt(n % half + 1)
        table[n, 8 + n // half * (mies // 2) + degree - 1] = 1.0
    table[dirs : dirs + boxes, :dirs] = np.cos(centre).T
    table[dirs + boxes :, :dirs] = np.sin(centre).T
    return table.astype(np.float32)


def iota(shape, dim):
    return lax.broadcasted_iota(jnp.int32, shape, dim)


def dot_nt(a, b):
    return lax.dot_general(a, b, (((1,), (1,)), ((), ())), preferred_element_type=F32)


def dot_nn(a, b):
    return jnp.dot(a, b, preferred_element_type=F32)


def kernel(
    n_x,
    n_y,
    table_ref,
    inc_ref,
    mie_ref,
    off_ref,
    box_ref,
    near_ref,
    src_ref,
    dst_ref,
    pat_ref,
    rec_ref,
    leaf_ref,
    fsrc_ref,
    fcls_ref,
    coarse_ref,
    sol_ref,
    res_ref,
    rows,
    leafs,
    cols,
    colsrc,
    sums,
    sumsrc,
    counts,
    y_ref,
    mief,
    cosT,
    sinT,
    chosen,
    pickhot,
    take,
    rows_send,
    rows_recv,
    leafs_send,
    leafs_recv,
    cols_send,
    cols_recv,
    sums_send,
    sums_recv,
):
    n = n_x * n_y
    coefs2, spheres = inc_ref.shape
    coefs = coefs2 // 2
    dirs = pat_ref.shape[1]
    boxes, list_len = fsrc_ref.shape
    classes, pairs = src_ref.shape
    leaf_classes = leaf_ref.shape[0]
    mies = mie_ref.shape[0] // 2
    px = lax.axis_index("bx")
    py = lax.axis_index("by")
    me = px * n_y + py

    barrier = pltpu.get_barrier_semaphore()

    def peer(step):
        other = lax.rem(me + step, n)
        return lax.div(other, n_y), lax.rem(other, n_y)

    def greet(step, carry):
        tx, ty = peer(step)
        pl.semaphore_signal(barrier, inc=1, device_id=(tx, ty), device_id_type=MESH)
        return carry

    lax.fori_loop(1, n, greet, 0)

    offsets = [(dx, dy) for dx in (-1, 0, 1) for dy in (-1, 0, 1)]
    around = [o for o in offsets if o != (0, 0)]
    own = 4

    def slot(dx, dy):
        return 3 * (dx + 1) + dy + 1

    def inside(dx, dy):
        tx, ty = px + dx, py + dy
        return (tx >= 0) & (tx < n_x) & (ty >= 0) & (ty < n_y)

    def row_block(it, s):
        return rows.at[it, :, pl.ds(s * spheres, spheres)]

    def leaf_block(it, s):
        return leafs.at[it, pl.ds(s * boxes, boxes), :]

    def block_copy(block, send, recv, it, dx, dy):
        return pltpu.make_async_remote_copy(
            src_ref=block(it, own),
            dst_ref=block(it, slot(-dx, -dy)),
            send_sem=send.at[it, slot(dx, dy)],
            recv_sem=recv.at[it, slot(-dx, -dy)],
            device_id=(px + dx, py + dy),
            device_id_type=MESH,
        )

    def arrival(block, send, recv, it, dx, dy):
        return pltpu.make_async_remote_copy(
            src_ref=block(it, own),
            dst_ref=block(it, slot(dx, dy)),
            send_sem=send.at[it, slot(dx, dy)],
            recv_sem=recv.at[it, slot(dx, dy)],
            device_id=(px + dx, py + dy),
            device_id_type=MESH,
        )

    def send_around(block, send, recv, it):
        for dx, dy in sorted(around, key=lambda o: -abs(o[0]) - abs(o[1])):
            @pl.when(inside(dx, dy))
            def _():
                block_copy(block, send, recv, it, dx, dy).start()

    def wait_around(block, send, recv, it):
        for dx, dy in around:
            @pl.when(inside(dx, dy))
            def _():
                arrival(block, send, recv, it, dx, dy).wait_recv()

    def wait_sent(block, send, recv, it):
        for dx, dy in around:
            @pl.when(inside(dx, dy))
            def _():
                block_copy(block, send, recv, it, dx, dy).wait_send()

    def send_all(src, dst, send, recv):
        def one(step, carry):
            tx, ty = peer(step)
            pltpu.make_async_remote_copy(
                src_ref=src,
                dst_ref=dst.at[me],
                send_sem=send,
                recv_sem=recv,
                device_id=(tx, ty),
                device_id_type=MESH,
            ).start()
            return carry

        lax.fori_loop(1, n, one, 0)

    def wait_bytes(dst, sem):
        view = dst.at[pl.ds(0, n - 1)]
        pltpu.make_async_copy(view, view, sem).wait()

    for it in range(2):
        for dx, dy in around:
            @pl.when(jnp.logical_not(inside(dx, dy)))
            def _():
                s = slot(dx, dy)
                rows[it, :, s * spheres : (s + 1) * spheres] = jnp.zeros((coefs2, spheres), BF16)
                leafs[it, s * boxes : (s + 1) * boxes, :] = jnp.zeros((boxes, 2 * dirs), BF16)

    incident = inc_ref[...]
    rows[0, :, own * spheres : (own + 1) * spheres] = incident.astype(BF16)

    phases = (
        table_ref[0:dirs, 0:1] * off_ref[0]
        + table_ref[0:dirs, 1:2] * off_ref[1]
        + table_ref[0:dirs, 2:3] * off_ref[2]
    )
    cos_s = jnp.cos(phases)
    sin_s = jnp.sin(phases)
    cos_b = table_ref[dirs : dirs + boxes, :]
    sin_b = table_ref[dirs + boxes : dirs + 2 * boxes, :]
    member = (iota((boxes, spheres), 0) == box_ref[...]).astype(F32).astype(BF16)
    member_t = (iota((LANES, spheres), 0) == box_ref[...]).astype(F32).T[:, :boxes].astype(BF16)
    pattern = pat_ref[...].reshape(2 * dirs, coefs)

    pl.semaphore_wait(barrier, n - 1)
    send_around(row_block, rows_send, rows_recv, 0)

    def outgoing(it):
        own_rows = rows[it, :, own * spheres : (own + 1) * spheres]
        wide = jnp.concatenate([own_rows[:coefs], own_rows[coefs:]], axis=1)
        sig = dot_nn(pattern, wide)
        sig_r = sig[:dirs, :spheres] - sig[dirs:, spheres:]
        sig_i = sig[dirs:, :spheres] + sig[:dirs, spheres:]
        out = jnp.concatenate(
            [sig_r * cos_s + sig_i * sin_s, sig_i * cos_s - sig_r * sin_s], axis=0
        )
        high = out.astype(BF16)
        low = (out - high.astype(F32)).astype(BF16)
        leaf_t = dot_nt(member, high) + dot_nt(member, low)
        leafs[it, own * boxes : (own + 1) * boxes, :] = leaf_t.astype(BF16)
        lr, li = leaf_t[:, :dirs], leaf_t[:, dirs:]
        up_r = jnp.sum(lr * cos_b + li * sin_b, axis=0, keepdims=True)
        up_i = jnp.sum(li * cos_b - lr * sin_b, axis=0, keepdims=True)
        colsrc[it] = jnp.concatenate([up_r, up_i], axis=0)
        send_all(colsrc.at[it], cols.at[it], cols_send.at[it], cols_recv.at[it])
        send_around(leaf_block, leafs_send, leafs_recv, it)

    outgoing(0)

    cosT[...] = cos_s.T
    sinT[...] = sin_s.T
    for c in range(2):
        mief[c] = jnp.dot(
            table_ref[0:coefs, 8 : 8 + mies],
            mie_ref[c * mies : (c + 1) * mies, :],
            precision=HIGHEST,
            preferred_element_type=F32,
        )
    take_r, take_i = rec_ref[0], rec_ref[1]
    take[...] = jnp.concatenate(
        [jnp.concatenate([take_r, -take_i], axis=1), jnp.concatenate([take_i, take_r], axis=1)],
        axis=0,
    )
    entries = boxes * list_len

    def entry_box(shape, dim):
        place = iota(shape, dim).astype(F32)
        return place, jnp.floor((place + 0.5) * (1.0 / list_len))

    place, its_box = entry_box((entries, boxes), 0)
    box_hot = (its_box == iota((entries, boxes), 1).astype(F32)).astype(F32)
    place, its_box = entry_box((entries, list_len), 0)
    list_hot = (place - list_len * its_box == iota((entries, list_len), 1).astype(F32)).astype(F32)

    def flat(ref):
        spread = jnp.dot(
            box_hot, ref[...].astype(F32), precision=HIGHEST, preferred_element_type=F32
        )
        return jnp.sum(spread * list_hot, axis=1, keepdims=True)

    nine = 9 * boxes
    pickhot[...] = (
        (flat(fsrc_ref) == iota((entries, nine), 1).astype(F32)).astype(F32).astype(BF16)
    )
    class_hot = (flat(fcls_ref) == iota((entries, leaf_classes), 1).astype(F32)).astype(F32)
    for c in range(2):
        chosen[c] = jnp.dot(
            class_hot, leaf_ref[:, c, :], precision=HIGHEST, preferred_element_type=F32
        )

    def count(pair, carry):
        for part in range(2):
            k = 2 * pair + part
            source = (iota((9 * spheres, pairs), 0) == src_ref[pl.ds(k, 1), :]).astype(F32)
            target = (iota((spheres, pairs), 0) == dst_ref[pl.ds(k, 1), :]).astype(F32)
            counts[pair, :, part * spheres : (part + 1) * spheres] = dot_nt(
                source.astype(BF16), target.astype(BF16)
            ).astype(BF16)
        return carry

    lax.fori_loop(0, classes // 2, count, 0)

    def incoming_field(it):
        wait_around(row_block, rows_send, rows_recv, it)

        def near_pair(pair, acc):
            gathered = dot_nn(rows[it], counts[pair])
            for part in range(2):
                one = gathered[:, part * spheres : (part + 1) * spheres].astype(BF16)
                wide = jnp.concatenate([one[:coefs], one[coefs:]], axis=1)
                acc = acc + dot_nn(near_ref[2 * pair + part], wide)
            return acc

        near = lax.fori_loop(
            0, classes // 2, near_pair, jnp.zeros((coefs2, 2 * spheres), F32)
        )
        near_r = near[:coefs, :spheres] - near[coefs:, spheres:]
        near_i = near[coefs:, :spheres] + near[:coefs, spheres:]

        wait_around(leaf_block, leafs_send, leafs_recv, it)
        picked = dot_nn(pickhot[...], leafs[it])
        pr, pi = picked[:, :dirs], picked[:, dirs:]
        cr, ci = chosen[0], chosen[1]
        leaf_r = jnp.sum((pr * cr - pi * ci).reshape(boxes, list_len, dirs), axis=1)
        leaf_i = jnp.sum((pr * ci + pi * cr).reshape(boxes, list_len, dirs), axis=1)

        wait_bytes(cols.at[it], cols_recv.at[it])
        cols[it, me] = colsrc[it]

        def column(i, acc):
            straight, crossed = acc
            x, y = lax.div(i, n_y), lax.rem(i, n_y)
            away = (jnp.abs(x - px) >= 2) | (jnp.abs(y - py) >= 2)
            weight = jnp.where(away, 1.0, 0.0)
            value = cols[it, i] * weight
            wr = coarse_ref[0, x + (n_x - 1) - px, pl.ds(y + (n_y - 1) - py, 1), :]
            wi = coarse_ref[1, x + (n_x - 1) - px, pl.ds(y + (n_y - 1) - py, 1), :]
            return straight + value * wr, crossed + value * wi

        zero = jnp.zeros((2, dirs), F32)
        straight, crossed = lax.fori_loop(0, n, column, (zero, zero), unroll=8)
        col_r = straight[0:1] - crossed[1:2]
        col_i = straight[1:2] + crossed[0:1]
        in_r = leaf_r + (col_r * cos_b - col_i * sin_b)
        in_i = leaf_i + (col_r * sin_b + col_i * cos_b)
        both = jnp.concatenate([in_r, in_i], axis=1)
        high = both.astype(BF16)
        low = (both - high.astype(F32)).astype(BF16)
        spread = dot_nn(member_t, high) + dot_nn(member_t, low)
        sr, si = spread[:, :dirs], spread[:, dirs:]
        ct, st = cosT[...], sinT[...]
        arriving = jnp.concatenate([sr * ct - si * st, sr * st + si * ct], axis=1).astype(BF16)
        far = dot_nt(take[...], arriving)
        fr = near_r + far[:coefs]
        fi = near_i + far[coefs:]
        mr, mi = mief[0], mief[1]
        return jnp.concatenate([fr * mr - fi * mi, fr * mi + fi * mr], axis=0)

    y = incoming_field(0)
    y_ref[...] = y
    rows[1, :, own * spheres : (own + 1) * spheres] = y.astype(BF16)
    send_around(row_block, rows_send, rows_recv, 1)
    outgoing(1)
    v = inc_ref[...]
    y = y_ref[...]

    def total(a, b):
        return jnp.sum(jnp.sum(a * b, axis=0, keepdims=True), axis=1, keepdims=True)

    g00, g01, g11 = total(v, v), total(v, y), total(y, y)
    z = incoming_field(1)
    v = inc_ref[...]
    y = y_ref[...]
    lane = iota((1, LANES), 1)
    row = jnp.zeros((1, LANES), F32)
    for i, value in enumerate((g00, g01, g11, total(v, z), total(y, z), total(z, z))):
        row = jnp.where(lane == i, value, row)
    sumsrc[...] = row
    send_all(sumsrc, sums, sums_send, sums_recv)
    wait_bytes(sums, sums_recv)
    sums[me] = row
    totals = jnp.sum(sums[...], axis=0)
    s00, s01, s11, s02, s12, s22 = (
        jnp.sum(jnp.where(lane == i, totals, 0.0), axis=1, keepdims=True) for i in range(6)
    )
    beta = jnp.sqrt(s00)
    a = s01 / s00
    h10 = jnp.sqrt((s11 - a * s01) / s00)
    g = 1.0 / (beta * h10)
    h00 = 1.0 - a
    d = (g / beta) * (a * s01 - s02)
    c = g * g * (a * (a * s01 - s02 - s11) + s12)
    e = g * g * (a * (a * s11 - 2.0 * s12) + s22)
    h21 = jnp.sqrt(e - c * c - d * d)
    h01 = -d
    h11 = 1.0 - c
    n11 = h00 * h00 + h10 * h10
    n12 = h00 * h01 + h10 * h11
    n22 = h01 * h01 + h11 * h11 + h21 * h21
    l11 = jnp.sqrt(n11)
    l21 = n12 / l11
    l22 = jnp.sqrt(n22 - l21 * l21)
    m0 = beta * h00 / l11
    m1 = (beta * h01 - l21 * m0) / l22
    w1 = m1 / l22
    w0 = (m0 - l21 * w1) / l11
    f0 = h00 * w0 + h01 * w1
    f1 = h10 * w0 + h11 * w1
    ga = g * a
    sol_ref[...] = (w0 / beta + w1 * ga) * v - (w1 * g) * y
    res_ref[...] = (
        ((beta - f0) / beta - f1 * ga - w1 * (d / beta + c * ga)) * v
        + (f1 * g + w1 * (ga + c * g)) * y
        - (w1 * g) * z
    )
    for it in range(2):
        wait_sent(row_block, rows_send, rows_recv, it)
        wait_sent(leaf_block, leafs_send, leafs_recv, it)
        wait_bytes(cols.at[it], cols_send.at[it])
    wait_bytes(sums, sums_send)


def local(n_x, n_y, *args):
    (
        incident,
        mie,
        offsets,
        sphere_box,
        near_table,
        near_src,
        near_dst,
        pattern,
        receive,
        leaf_transfer,
        far_src,
        far_cls,
        coarse_transfer,
    ) = args
    coefs = incident.shape[1]
    spheres = incident.shape[4]
    mies = mie.shape[1]
    dirs = pattern.shape[1]
    boxes, list_len = far_src.shape[2:]
    classes, pairs = near_src.shape[2:]
    n = n_x * n_y
    coefs2 = 2 * coefs
    entries = boxes * list_len
    table = jnp.asarray(constants(dirs, boxes, coefs, mies))
    vmem = pl.BlockSpec(memory_space=pltpu.VMEM)
    shape = jax.ShapeDtypeStruct((coefs2, spheres), F32)
    dma = pltpu.SemaphoreType.DMA
    sol, res = pl.pallas_call(
        functools.partial(kernel, n_x, n_y),
        out_shape=(shape, shape),
        in_specs=[vmem] * 14,
        out_specs=(vmem, vmem),
        scratch_shapes=[
            pltpu.VMEM((2, coefs2, 9 * spheres), BF16),
            pltpu.VMEM((2, 9 * boxes, 2 * dirs), BF16),
            pltpu.VMEM((2, n, 2, dirs), F32),
            pltpu.VMEM((2, 2, dirs), F32),
            pltpu.VMEM((n, 1, LANES), F32),
            pltpu.VMEM((1, LANES), F32),
            pltpu.VMEM((classes // 2, 9 * spheres, 2 * spheres), BF16),
            pltpu.VMEM((coefs2, spheres), F32),
            pltpu.VMEM((2, coefs, spheres), F32),
            pltpu.VMEM((spheres, dirs), F32),
            pltpu.VMEM((spheres, dirs), F32),
            pltpu.VMEM((2, entries, dirs), F32),
            pltpu.VMEM((entries, 9 * boxes), BF16),
            pltpu.VMEM((coefs2, 2 * dirs), BF16),
            dma((2, 9)),
            dma((2, 9)),
            dma((2, 9)),
            dma((2, 9)),
            dma((2,)),
            dma((2,)),
            dma,
            dma,
        ],
        compiler_params=pltpu.CompilerParams(
            collective_id=0, has_side_effects=True, vmem_limit_bytes=60 * 1024 * 1024
        ),
    )(
        table,
        incident.reshape(coefs2, spheres),
        mie.reshape(2 * mies, spheres),
        offsets.reshape(3, 1, spheres),
        sphere_box.reshape(1, spheres),
        near_table.reshape(classes, coefs2, coefs),
        near_src.reshape(classes, pairs),
        near_dst.reshape(classes, pairs),
        pattern,
        receive,
        leaf_transfer,
        far_src.reshape(boxes, list_len),
        far_cls.reshape(boxes, list_len),
        coarse_transfer,
    )
    return sol.reshape(incident.shape), res.reshape(incident.shape)


def solution(mesh):
    field = P(None, None, "bx", "by", None)
    placed = (
        field,
        field,
        P(None, "bx", "by", None),
        P("bx", "by", None),
        P(),
        P("bx", "by", None, None),
        P("bx", "by", None, None),
        P(),
        P(),
        P(),
        P("bx", "by", None, None),
        P("bx", "by", None, None),
        P(),
    )
    return jax.shard_map(
        functools.partial(local, mesh.shape["bx"], mesh.shape["by"]),
        mesh=mesh,
        in_specs=placed,
        out_specs=(field, field),
        check_vma=False,
    )
```

```python
import functools
import math

import jax
import jax.numpy as jnp
import numpy as np
from jax import lax
from jax.experimental import pallas as pl
from jax.experimental.pallas import tpu as pltpu
from jax.sharding import PartitionSpec as P

KAPPA = 1.5
GOLDEN = 2.399963229728653
HIGHEST = lax.Precision.HIGHEST
F32 = jnp.float32
BF16 = jnp.bfloat16
MESH = pl.DeviceIdType.MESH
LANES = 128
EARLY = 3


def constants(dirs, boxes, coefs, mies):
    q = np.arange(dirs, dtype=np.float64)
    height = 1.0 - (2.0 * q + 1.0) / dirs
    radius = np.sqrt(1.0 - height * height)
    planes = np.stack([radius * np.cos(GOLDEN * q), radius * np.sin(GOLDEN * q), height], axis=1)
    b = np.arange(boxes)
    centers = np.stack([2.0 * (b % 2) - 1.0, 2.0 * (b // 2 % 2) - 1.0, 2.0 * (b // 4) - (boxes // 4 - 1)])
    centre = KAPPA * (planes @ centers)
    table = np.zeros((dirs + 2 * boxes, LANES), np.float64)
    table[:dirs, :3] = KAPPA * planes
    half = coefs // 2
    for n in range(coefs):
        degree = math.isqrt(n % half + 1)
        table[n, 8 + n // half * (mies // 2) + degree - 1] = 1.0
    table[dirs : dirs + boxes, :dirs] = np.cos(centre).T
    table[dirs + boxes :, :dirs] = np.sin(centre).T
    return table.astype(np.float32)


def iota(shape, dim):
    return lax.broadcasted_iota(jnp.int32, shape, dim)


def dot_nt(a, b):
    return lax.dot_general(a, b, (((1,), (1,)), ((), ())), preferred_element_type=F32)


def dot_nn(a, b):
    return jnp.dot(a, b, preferred_element_type=F32)


def kernel(
    n_x,
    n_y,
    table_hbm,
    inc_hbm,
    mie_hbm,
    off_hbm,
    box_hbm,
    near_hbm,
    src_hbm,
    dst_hbm,
    pat_hbm,
    rec_hbm,
    leaf_hbm,
    fsrc_hbm,
    fcls_hbm,
    coarse_hbm,
    sol_ref,
    res_ref,
    table_ref,
    inc_ref,
    mie_ref,
    off_ref,
    box_ref,
    near_ref,
    src_ref,
    dst_ref,
    pat_ref,
    rec_ref,
    leaf_ref,
    fsrc_ref,
    fcls_ref,
    coarse_ref,
    in_sems,
    rows,
    leafs,
    cols,
    colsrc,
    sums,
    sumsrc,
    counts,
    y_ref,
    mief,
    cosT,
    sinT,
    chosen,
    pickhot,
    take,
    send_pat,
    tcat,
    gcat,
    near_acc,
    rows_send,
    rows_recv,
    leafs_send,
    leafs_recv,
    cols_send,
    cols_recv,
    sums_send,
    sums_recv,
):
    n = n_x * n_y
    coefs2, spheres = inc_ref.shape
    coefs = coefs2 // 2
    dirs = pat_ref.shape[2]
    boxes, list_len = fsrc_ref.shape
    classes, pairs = src_ref.shape
    leaf_classes = leaf_ref.shape[0]
    mies = mie_ref.shape[0] // 2
    px = lax.axis_index("bx")
    py = lax.axis_index("by")
    me = px * n_y + py

    loads = {}
    pairs_in = (
        ("table", table_hbm, table_ref),
        ("inc", inc_hbm, inc_ref),
        ("off", off_hbm, off_ref),
        ("box", box_hbm, box_ref),
        ("pat", pat_hbm, pat_ref),
        ("fsrc", fsrc_hbm, fsrc_ref),
        ("fcls", fcls_hbm, fcls_ref),
        ("src", src_hbm, src_ref),
        ("dst", dst_hbm, dst_ref),
        ("near", near_hbm, near_ref),
        ("leaf", leaf_hbm, leaf_ref),
        ("mie", mie_hbm, mie_ref),
        ("rec", rec_hbm, rec_ref),
        ("coarse", coarse_hbm, coarse_ref),
    )
    for i, (name, source, target) in enumerate(pairs_in):
        loads[name] = pltpu.make_async_copy(source, target, in_sems.at[i])
        loads[name].start()

    def ready(*wanted):
        for name in wanted:
            loads[name].wait()

    barrier = pltpu.get_barrier_semaphore()

    def peer(step):
        other = lax.rem(me + step, n)
        return lax.div(other, n_y), lax.rem(other, n_y)

    def greet(step, carry):
        tx, ty = peer(step)
        pl.semaphore_signal(barrier, inc=1, device_id=(tx, ty), device_id_type=MESH)
        return carry

    lax.fori_loop(1, n, greet, 0)

    offsets = [(dx, dy) for dx in (-1, 0, 1) for dy in (-1, 0, 1)]
    around = [o for o in offsets if o != (0, 0)]
    own = 4

    def slot(dx, dy):
        return 3 * (dx + 1) + dy + 1

    order = [(0, -1), (0, 0), (0, 1), (-1, 0), (1, 0), (-1, -1), (-1, 1), (1, -1), (1, 1)]
    places = {slot(*o): i for i, o in enumerate(order)}
    mates = n_y % 2 == 0
    mate = 1 - 2 * lax.rem(py, 2)

    def direct(dx, dy):
        if not mates or dx == 0 or dy == 0:
            return inside(dx, dy)
        return inside(dx, dy) & (mate != dy)

    def inside(dx, dy):
        tx, ty = px + dx, py + dy
        return (tx >= 0) & (tx < n_x) & (ty >= 0) & (ty < n_y)

    def row_block(it, s):
        return rows.at[it, :, pl.ds(places[s] * spheres, spheres)]

    def leaf_block(it, s):
        return leafs.at[it, pl.ds(s * boxes, boxes), :]

    def block_copy(block, send, recv, it, dx, dy):
        return pltpu.make_async_remote_copy(
            src_ref=block(it, own),
            dst_ref=block(it, slot(-dx, -dy)),
            send_sem=send.at[it, slot(dx, dy)],
            recv_sem=recv.at[it, slot(-dx, -dy)],
            device_id=(px + dx, py + dy),
            device_id_type=MESH,
        )

    def arrival(block, send, recv, it, dx, dy):
        return pltpu.make_async_remote_copy(
            src_ref=block(it, own),
            dst_ref=block(it, slot(dx, dy)),
            send_sem=send.at[it, slot(dx, dy)],
            recv_sem=recv.at[it, slot(dx, dy)],
            device_id=(px + dx, py + dy),
            device_id_type=MESH,
        )

    def send_to(which, block, send, recv, it, allowed=inside):
        for dx, dy in which:
            @pl.when(allowed(dx, dy))
            def _():
                block_copy(block, send, recv, it, dx, dy).start()

    def wait_from(which, block, send, recv, it):
        for dx, dy in which:
            @pl.when(inside(dx, dy))
            def _():
                arrival(block, send, recv, it, dx, dy).wait_recv()

    def wait_sent(block, send, recv, it, allowed=inside):
        for dx, dy in around:
            @pl.when(allowed(dx, dy))
            def _():
                block_copy(block, send, recv, it, dx, dy).wait_send()

    def relays(it, act):
        if not mates:
            return
        for dx in (-1, 1):
            for dm in (-1, 1):
                @pl.when(inside(dx, 0) & (mate == dm))
                def _():
                    act(
                        pltpu.make_async_remote_copy(
                            src_ref=row_block(it, slot(dx, 0)),
                            dst_ref=row_block(it, slot(dx, -dm)),
                            send_sem=rows_send.at[it, slot(dx, dm)],
                            recv_sem=rows_recv.at[it, slot(dx, -dm)],
                            device_id=(px, py + dm),
                            device_id_type=MESH,
                        )
                    )

    def send_all(src, dst, send, recv):
        def one(step, carry):
            tx, ty = peer(step)
            pltpu.make_async_remote_copy(
                src_ref=src,
                dst_ref=dst.at[me],
                send_sem=send,
                recv_sem=recv,
                device_id=(tx, ty),
                device_id_type=MESH,
            ).start()
            return carry

        lax.fori_loop(1, n, one, 0)

    def wait_bytes(dst, sem):
        view = dst.at[pl.ds(0, n - 1)]
        pltpu.make_async_copy(view, view, sem).wait()

    for it in range(2):
        for dx, dy in around:
            @pl.when(jnp.logical_not(inside(dx, dy)))
            def _():
                s = slot(dx, dy)
                p = places[s]
                rows[it, :, p * spheres : (p + 1) * spheres] = jnp.zeros((coefs2, spheres), BF16)
                leafs[it, s * boxes : (s + 1) * boxes, :] = jnp.zeros((boxes, 2 * dirs), BF16)

    mid = places[own]
    ready("table", "inc", "off", "box", "pat")
    rows[0, :, mid * spheres : (mid + 1) * spheres] = inc_ref[...].astype(BF16)

    phases = (
        table_ref[0:dirs, 0:1] * off_ref[0]
        + table_ref[0:dirs, 1:2] * off_ref[1]
        + table_ref[0:dirs, 2:3] * off_ref[2]
    )
    cos_s = jnp.cos(phases)
    sin_s = jnp.sin(phases)
    cos_b = table_ref[dirs : dirs + boxes, :]
    sin_b = table_ref[dirs + boxes : dirs + 2 * boxes, :]
    member = (iota((boxes, spheres), 0) == box_ref[...]).astype(F32).astype(BF16)
    member_t = (iota((LANES, spheres), 0) == box_ref[...]).astype(F32).T[:, :boxes].astype(BF16)
    for c in range(2):
        send_pat[c * dirs : (c + 1) * dirs, :] = pat_ref[c].astype(F32).T.astype(BF16)

    z_rows = [(-1, 0), (1, 0)]
    y_rows = [(0, -1), (0, 1)]
    corners = [(-1, -1), (-1, 1), (1, -1), (1, 1)]
    row_args = (row_block, rows_send, rows_recv)
    leaf_args = (leaf_block, leafs_send, leafs_recv)

    def outgoing(it):
        own_rows = rows[it, :, mid * spheres : (mid + 1) * spheres]
        wide = jnp.concatenate([own_rows[:coefs], own_rows[coefs:]], axis=1)
        sig = dot_nn(send_pat[...], wide)
        sig_r = sig[:dirs, :spheres] - sig[dirs:, spheres:]
        sig_i = sig[dirs:, :spheres] + sig[:dirs, spheres:]
        out = jnp.concatenate(
            [sig_r * cos_s + sig_i * sin_s, sig_i * cos_s - sig_r * sin_s], axis=0
        )
        high = out.astype(BF16)
        low = (out - high.astype(F32)).astype(BF16)
        leaf_t = dot_nt(member, high) + dot_nt(member, low)
        leafs[it, own * boxes : (own + 1) * boxes, :] = leaf_t.astype(BF16)
        lr, li = leaf_t[:, :dirs], leaf_t[:, dirs:]
        up_r = jnp.sum(lr * cos_b + li * sin_b, axis=0, keepdims=True)
        up_i = jnp.sum(li * cos_b - lr * sin_b, axis=0, keepdims=True)
        colsrc[it] = jnp.concatenate([up_r, up_i], axis=0)

    def send_rest(it):
        send_all(colsrc.at[it], cols.at[it], cols_send.at[it], cols_recv.at[it])
        send_to(around, *leaf_args, it)
        send_to(corners, *row_args, it, direct)
        send_to(y_rows, *row_args, it)

    outgoing(0)

    cosT[...] = cos_s.T
    sinT[...] = sin_s.T
    ready("mie", "rec", "leaf", "fsrc", "fcls", "src", "dst")
    for c in range(2):
        mief[c] = jnp.dot(
            table_ref[0:coefs, 8 : 8 + mies],
            mie_ref[c * mies : (c + 1) * mies, :],
            precision=HIGHEST,
            preferred_element_type=F32,
        )
    take_r, take_i = rec_ref[0], rec_ref[1]
    take[...] = jnp.concatenate(
        [jnp.concatenate([take_r, -take_i], axis=1), jnp.concatenate([take_i, take_r], axis=1)],
        axis=0,
    )
    entries = boxes * list_len

    def entry_box(shape, dim):
        place = iota(shape, dim).astype(F32)
        return place, jnp.floor((place + 0.5) * (1.0 / list_len))

    place, its_box = entry_box((entries, boxes), 0)
    box_hot = (its_box == iota((entries, boxes), 1).astype(F32)).astype(F32)
    place, its_box = entry_box((entries, list_len), 0)
    list_hot = (place - list_len * its_box == iota((entries, list_len), 1).astype(F32)).astype(F32)

    def flat(ref):
        spread = jnp.dot(
            box_hot, ref[...].astype(F32), precision=HIGHEST, preferred_element_type=F32
        )
        return jnp.sum(spread * list_hot, axis=1, keepdims=True)

    nine = 9 * boxes
    pickhot[...] = (
        (flat(fsrc_ref) == iota((entries, nine), 1).astype(F32)).astype(F32).astype(BF16)
    )
    class_hot = (flat(fcls_ref) == iota((entries, leaf_classes), 1).astype(F32)).astype(F32)
    for c in range(2):
        chosen[c] = jnp.dot(
            class_hot, leaf_ref[:, c, :], precision=HIGHEST, preferred_element_type=F32
        )

    def count(pair, carry):
        here = iota((spheres, pairs), 0)
        for part in range(2):
            k = 2 * pair + part
            src = src_ref[pl.ds(k, 1), :]
            source = jnp.concatenate(
                [(here == src - slot(*o) * spheres).astype(F32).astype(BF16) for o in order], axis=0
            )
            target = (here == dst_ref[pl.ds(k, 1), :]).astype(F32).astype(BF16)
            counts[pair, :, part * spheres : (part + 1) * spheres] = dot_nt(source, target).astype(
                BF16
            )
        return carry

    early = EARLY * classes // 16
    lax.fori_loop(0, early, count, 0)

    pl.semaphore_wait(barrier, n - 1)
    send_to(z_rows, *row_args, 0)
    send_rest(0)

    lax.fori_loop(early, classes // 2, count, 0)
    ready("near", "coarse")
    tcat[...] = jnp.zeros(tcat.shape, BF16)
    gcat[...] = jnp.zeros(gcat.shape, BF16)
    for k in range(classes):
        tcat[:, k * LANES : k * LANES + coefs] = near_ref[k]

    def near_group(it, first, last, start):
        low, high = first * spheres, last * spheres

        def near_pair(pair, carry):
            gathered = dot_nn(rows[it, :, low:high], counts[pair, low:high, :]).astype(BF16)
            for part in range(2):
                one = gathered[:, part * spheres : (part + 1) * spheres]
                wide = jnp.concatenate([one[:coefs], one[coefs:]], axis=1)
                base = pl.multiple_of((2 * pair + part) * LANES, LANES)
                gcat[pl.ds(base, coefs), :] = wide
            return carry

        lax.fori_loop(0, classes // 2, near_pair, 0, unroll=2)
        total = dot_nn(tcat[...], gcat[...])
        near_acc[...] = total if start else near_acc[...] + total

    def incoming_field(it):
        wait_from(y_rows, *row_args, it)
        near_group(it, 0, 3, True)
        wait_from(z_rows, *row_args, it)
        relays(it, lambda copy: copy.start())
        near_group(it, 3, 5, False)

        wait_from(around, *leaf_args, it)
        picked = dot_nn(pickhot[...], leafs[it])
        pr, pi = picked[:, :dirs], picked[:, dirs:]
        cr, ci = chosen[0], chosen[1]
        leaf_r = jnp.sum((pr * cr - pi * ci).reshape(boxes, list_len, dirs), axis=1)
        leaf_i = jnp.sum((pr * ci + pi * cr).reshape(boxes, list_len, dirs), axis=1)

        wait_bytes(cols.at[it], cols_recv.at[it])
        cols[it, me] = colsrc[it]

        def column(i, acc):
            straight, crossed = acc
            x, y = lax.div(i, n_y), lax.rem(i, n_y)
            away = (jnp.abs(x - px) >= 2) | (jnp.abs(y - py) >= 2)
            weight = jnp.where(away, 1.0, 0.0)
            value = cols[it, i] * weight
            w = coarse_ref[x + (n_x - 1) - px, y + (n_y - 1) - py]
            return straight + value * w[0:1], crossed + value * w[1:2]

        zero = jnp.zeros((2, dirs), F32)
        straight, crossed = lax.fori_loop(0, n, column, (zero, zero), unroll=8)
        col_r = straight[0:1] - crossed[1:2]
        col_i = straight[1:2] + crossed[0:1]
        in_r = leaf_r + (col_r * cos_b - col_i * sin_b)
        in_i = leaf_i + (col_r * sin_b + col_i * cos_b)
        both = jnp.concatenate([in_r, in_i], axis=1)
        high = both.astype(BF16)
        low = (both - high.astype(F32)).astype(BF16)
        spread = dot_nn(member_t, high) + dot_nn(member_t, low)
        sr, si = spread[:, :dirs], spread[:, dirs:]
        ct, st = cosT[...], sinT[...]
        arriving = jnp.concatenate([sr * ct - si * st, sr * st + si * ct], axis=1).astype(BF16)
        far = dot_nt(take[...], arriving)
        wait_from(corners, *row_args, it)
        near_group(it, 5, 9, False)
        near = near_acc[...]
        near_r = near[:coefs, :spheres] - near[coefs:, spheres:]
        near_i = near[coefs:, :spheres] + near[:coefs, spheres:]
        fr = near_r + far[:coefs]
        fi = near_i + far[coefs:]
        mr, mi = mief[0], mief[1]
        return jnp.concatenate([fr * mr - fi * mi, fr * mi + fi * mr], axis=0)

    y = incoming_field(0)
    y_ref[...] = y
    rows[1, :, mid * spheres : (mid + 1) * spheres] = y.astype(BF16)
    send_to(z_rows, *row_args, 1)
    outgoing(1)
    send_rest(1)
    v = inc_ref[...]
    y = y_ref[...]

    def total(a, b):
        return jnp.sum(jnp.sum(a * b, axis=0, keepdims=True), axis=1, keepdims=True)

    g00, g01, g11 = total(v, v), total(v, y), total(y, y)
    z = incoming_field(1)
    v = inc_ref[...]
    y = y_ref[...]
    lane = iota((1, LANES), 1)
    row = jnp.zeros((1, LANES), F32)
    for i, value in enumerate((g00, g01, g11, total(v, z), total(y, z), total(z, z))):
        row = jnp.where(lane == i, value, row)
    sumsrc[...] = row
    send_all(sumsrc, sums, sums_send, sums_recv)
    wait_bytes(sums, sums_recv)
    sums[me] = row
    totals = jnp.sum(sums[...], axis=0)
    s00, s01, s11, s02, s12, s22 = (
        jnp.sum(jnp.where(lane == i, totals, 0.0), axis=1, keepdims=True) for i in range(6)
    )
    beta = jnp.sqrt(s00)
    a = s01 / s00
    h10 = jnp.sqrt((s11 - a * s01) / s00)
    g = 1.0 / (beta * h10)
    h00 = 1.0 - a
    d = (g / beta) * (a * s01 - s02)
    c = g * g * (a * (a * s01 - s02 - s11) + s12)
    e = g * g * (a * (a * s11 - 2.0 * s12) + s22)
    h21 = jnp.sqrt(e - c * c - d * d)
    h01 = -d
    h11 = 1.0 - c
    n11 = h00 * h00 + h10 * h10
    n12 = h00 * h01 + h10 * h11
    n22 = h01 * h01 + h11 * h11 + h21 * h21
    l11 = jnp.sqrt(n11)
    l21 = n12 / l11
    l22 = jnp.sqrt(n22 - l21 * l21)
    m0 = beta * h00 / l11
    m1 = (beta * h01 - l21 * m0) / l22
    w1 = m1 / l22
    w0 = (m0 - l21 * w1) / l11
    f0 = h00 * w0 + h01 * w1
    f1 = h10 * w0 + h11 * w1
    ga = g * a
    sol_ref[...] = (w0 / beta + w1 * ga) * v - (w1 * g) * y
    res_ref[...] = (
        ((beta - f0) / beta - f1 * ga - w1 * (d / beta + c * ga)) * v
        + (f1 * g + w1 * (ga + c * g)) * y
        - (w1 * g) * z
    )
    for it in range(2):
        wait_sent(*row_args, it, direct)
        relays(it, lambda copy: copy.wait_send())
        wait_sent(*leaf_args, it)
        wait_bytes(cols.at[it], cols_send.at[it])
    wait_bytes(sums, sums_send)


def local(n_x, n_y, *args):
    (
        incident,
        mie,
        offsets,
        sphere_box,
        near_table,
        near_src,
        near_dst,
        pattern,
        receive,
        leaf_transfer,
        far_src,
        far_cls,
        coarse_transfer,
    ) = args
    coefs = incident.shape[1]
    spheres = incident.shape[4]
    mies = mie.shape[1]
    dirs = pattern.shape[1]
    pat_t = pattern.transpose(0, 2, 1)
    coarse_t = coarse_transfer.transpose(1, 2, 0, 3)
    boxes, list_len = far_src.shape[2:]
    classes, pairs = near_src.shape[2:]
    n = n_x * n_y
    coefs2 = 2 * coefs
    entries = boxes * list_len
    table = jnp.asarray(constants(dirs, boxes, coefs, mies))
    operands = (
        table,
        incident.reshape(coefs2, spheres),
        mie.reshape(2 * mies, spheres),
        offsets.reshape(3, 1, spheres),
        sphere_box.reshape(1, spheres),
        near_table.reshape(classes, coefs2, coefs),
        near_src.reshape(classes, pairs),
        near_dst.reshape(classes, pairs),
        pat_t,
        receive,
        leaf_transfer,
        far_src.reshape(boxes, list_len),
        far_cls.reshape(boxes, list_len),
        coarse_t,
    )
    vmem = pl.BlockSpec(memory_space=pltpu.VMEM)
    shape = jax.ShapeDtypeStruct((coefs2, spheres), F32)
    dma = pltpu.SemaphoreType.DMA
    sol, res = pl.pallas_call(
        functools.partial(kernel, n_x, n_y),
        out_shape=(shape, shape),
        in_specs=[pl.BlockSpec(memory_space=pltpu.HBM)] * len(operands),
        out_specs=(vmem, vmem),
        scratch_shapes=[pltpu.VMEM(x.shape, x.dtype) for x in operands]
        + [
            dma((len(operands),)),
            pltpu.VMEM((2, coefs2, 9 * spheres), BF16),
            pltpu.VMEM((2, 9 * boxes, 2 * dirs), BF16),
            pltpu.VMEM((2, n, 2, dirs), F32),
            pltpu.VMEM((2, 2, dirs), F32),
            pltpu.VMEM((n, 1, LANES), F32),
            pltpu.VMEM((1, LANES), F32),
            pltpu.VMEM((classes // 2, 9 * spheres, 2 * spheres), BF16),
            pltpu.VMEM((coefs2, spheres), F32),
            pltpu.VMEM((2, coefs, spheres), F32),
            pltpu.VMEM((spheres, dirs), F32),
            pltpu.VMEM((spheres, dirs), F32),
            pltpu.VMEM((2, entries, dirs), F32),
            pltpu.VMEM((entries, 9 * boxes), BF16),
            pltpu.VMEM((coefs2, 2 * dirs), BF16),
            pltpu.VMEM((2 * dirs, coefs), BF16),
            pltpu.VMEM((coefs2, classes * LANES), BF16),
            pltpu.VMEM((classes * LANES, 2 * spheres), BF16),
            pltpu.VMEM((coefs2, 2 * spheres), F32),
            dma((2, 9)),
            dma((2, 9)),
            dma((2, 9)),
            dma((2, 9)),
            dma((2,)),
            dma((2,)),
            dma,
            dma,
        ],
        compiler_params=pltpu.CompilerParams(
            collective_id=0, has_side_effects=True, vmem_limit_bytes=24 * 1024 * 1024
        ),
    )(*operands)
    return sol.reshape(incident.shape), res.reshape(incident.shape)


def solution(mesh):
    field = P(None, None, "bx", "by", None)
    placed = (
        field,
        field,
        P(None, "bx", "by", None),
        P("bx", "by", None),
        P(),
        P("bx", "by", None, None),
        P("bx", "by", None, None),
        P(),
        P(),
        P(),
        P("bx", "by", None, None),
        P("bx", "by", None, None),
        P(),
    )
    return jax.shard_map(
        functools.partial(local, mesh.shape["bx"], mesh.shape["by"]),
        mesh=mesh,
        in_specs=placed,
        out_specs=(field, field),
        check_vma=False,
    )
```

```python
import functools
import math

import jax
import jax.numpy as jnp
import numpy as np
from jax import lax
from jax.experimental import pallas as pl
from jax.experimental.pallas import tpu as pltpu
from jax.sharding import PartitionSpec as P

KAPPA = 1.5
GOLDEN = 2.399963229728653
HIGHEST = lax.Precision.HIGHEST
F32 = jnp.float32
BF16 = jnp.bfloat16
MESH = pl.DeviceIdType.MESH
LANES = 128


def constants(dirs, boxes, coefs, mies):
    q = np.arange(dirs, dtype=np.float64)
    height = 1.0 - (2.0 * q + 1.0) / dirs
    radius = np.sqrt(1.0 - height * height)
    planes = np.stack([radius * np.cos(GOLDEN * q), radius * np.sin(GOLDEN * q), height], axis=1)
    b = np.arange(boxes)
    centers = np.stack([2.0 * (b % 2) - 1.0, 2.0 * (b // 2 % 2) - 1.0, 2.0 * (b // 4) - (boxes // 4 - 1)])
    centre = KAPPA * (planes @ centers)
    table = np.zeros((dirs + 2 * boxes, LANES), np.float64)
    table[:dirs, :3] = KAPPA * planes
    half = coefs // 2
    for n in range(coefs):
        degree = math.isqrt(n % half + 1)
        table[n, 8 + n // half * (mies // 2) + degree - 1] = 1.0
    table[dirs : dirs + boxes, :dirs] = np.cos(centre).T
    table[dirs + boxes :, :dirs] = np.sin(centre).T
    return table.astype(np.float32)


def iota(shape, dim):
    return lax.broadcasted_iota(jnp.int32, shape, dim)


def dot_nt(a, b):
    return lax.dot_general(a, b, (((1,), (1,)), ((), ())), preferred_element_type=F32)


def dot_nn(a, b):
    return jnp.dot(a, b, preferred_element_type=F32)


def kernel(
    n_x,
    n_y,
    table_hbm,
    inc_hbm,
    mie_hbm,
    off_hbm,
    box_hbm,
    near_hbm,
    src_hbm,
    dst_hbm,
    pat_hbm,
    rec_hbm,
    leaf_hbm,
    fsrc_hbm,
    fcls_hbm,
    coarse_hbm,
    sol_ref,
    res_ref,
    table_ref,
    inc_ref,
    mie_ref,
    off_ref,
    box_ref,
    near_ref,
    src_ref,
    dst_ref,
    pat_ref,
    rec_ref,
    leaf_ref,
    fsrc_ref,
    fcls_ref,
    coarse_ref,
    in_sems,
    rows,
    leafs,
    cols,
    colsrc,
    sums,
    sumsrc,
    counts,
    y_ref,
    mief,
    cosT,
    sinT,
    chosen,
    pickhot,
    take,
    send_pat,
    tcat,
    gcat,
    near_acc,
    rows_send,
    rows_recv,
    leafs_send,
    leafs_recv,
    cols_send,
    cols_recv,
    sums_send,
    sums_recv,
):
    n = n_x * n_y
    coefs2, spheres = inc_ref.shape
    coefs = coefs2 // 2
    dirs = pat_ref.shape[2]
    boxes, list_len = fsrc_ref.shape
    classes, pairs = src_ref.shape
    leaf_classes = leaf_ref.shape[0]
    mies = mie_ref.shape[0] // 2
    px = lax.axis_index("bx")
    py = lax.axis_index("by")
    me = px * n_y + py

    loads = {}
    pairs_in = (
        ("table", table_hbm, table_ref),
        ("inc", inc_hbm, inc_ref),
        ("off", off_hbm, off_ref),
        ("box", box_hbm, box_ref),
        ("pat", pat_hbm, pat_ref),
        ("fsrc", fsrc_hbm, fsrc_ref),
        ("fcls", fcls_hbm, fcls_ref),
        ("src", src_hbm, src_ref),
        ("dst", dst_hbm, dst_ref),
        ("near", near_hbm, near_ref),
        ("leaf", leaf_hbm, leaf_ref),
        ("mie", mie_hbm, mie_ref),
        ("rec", rec_hbm, rec_ref),
        ("coarse", coarse_hbm, coarse_ref),
    )
    for i, (name, source, target) in enumerate(pairs_in):
        loads[name] = pltpu.make_async_copy(source, target, in_sems.at[i])
        loads[name].start()

    def ready(*wanted):
        for name in wanted:
            loads[name].wait()

    barrier = pltpu.get_barrier_semaphore()

    def peer(step):
        other = lax.rem(me + step, n)
        return lax.div(other, n_y), lax.rem(other, n_y)

    def greet(step, carry):
        tx, ty = peer(step)
        pl.semaphore_signal(barrier, inc=1, device_id=(tx, ty), device_id_type=MESH)
        return carry

    fold = max(d for d in range(1, 32) if (n - 1) % d == 0)
    lax.fori_loop(1, n, greet, 0, unroll=fold)

    offsets = [(dx, dy) for dx in (-1, 0, 1) for dy in (-1, 0, 1)]
    around = [o for o in offsets if o != (0, 0)]
    own = 4

    def slot(dx, dy):
        return 3 * (dx + 1) + dy + 1

    order = [(0, -1), (0, 0), (0, 1), (-1, 0), (1, 0), (-1, -1), (-1, 1), (1, -1), (1, 1)]
    places = {slot(*o): i for i, o in enumerate(order)}

    def inside(dx, dy):
        tx, ty = px + dx, py + dy
        return (tx >= 0) & (tx < n_x) & (ty >= 0) & (ty < n_y)

    def row_block(it, s):
        return rows.at[it, :, pl.ds(places[s] * spheres, spheres)]

    def leaf_block(it, s):
        return leafs.at[it, pl.ds(s * boxes, boxes), :]

    def block_copy(block, send, recv, it, dx, dy):
        return pltpu.make_async_remote_copy(
            src_ref=block(it, own),
            dst_ref=block(it, slot(-dx, -dy)),
            send_sem=send.at[it, slot(dx, dy)],
            recv_sem=recv.at[it, slot(-dx, -dy)],
            device_id=(px + dx, py + dy),
            device_id_type=MESH,
        )

    def arrival(block, send, recv, it, dx, dy):
        return pltpu.make_async_remote_copy(
            src_ref=block(it, own),
            dst_ref=block(it, slot(dx, dy)),
            send_sem=send.at[it, slot(dx, dy)],
            recv_sem=recv.at[it, slot(dx, dy)],
            device_id=(px + dx, py + dy),
            device_id_type=MESH,
        )

    def send_to(which, block, send, recv, it, allowed=inside):
        for dx, dy in which:
            @pl.when(allowed(dx, dy))
            def _():
                block_copy(block, send, recv, it, dx, dy).start()

    def wait_from(which, block, send, recv, it):
        for dx, dy in which:
            @pl.when(inside(dx, dy))
            def _():
                arrival(block, send, recv, it, dx, dy).wait_recv()

    def wait_sent(block, send, recv, it, allowed=inside):
        for dx, dy in around:
            @pl.when(allowed(dx, dy))
            def _():
                block_copy(block, send, recv, it, dx, dy).wait_send()

    def send_all(src, dst, send, recv):
        def one(step, carry):
            tx, ty = peer(step)
            pltpu.make_async_remote_copy(
                src_ref=src,
                dst_ref=dst.at[me],
                send_sem=send,
                recv_sem=recv,
                device_id=(tx, ty),
                device_id_type=MESH,
            ).start()
            return carry

        lax.fori_loop(1, n, one, 0, unroll=fold)

    def wait_bytes(dst, sem):
        view = dst.at[pl.ds(0, n - 1)]
        pltpu.make_async_copy(view, view, sem).wait()

    mid = places[own]
    ready("table", "inc", "off", "box", "pat")
    rows[0, :, mid * spheres : (mid + 1) * spheres] = inc_ref[...].astype(BF16)

    phases = (
        table_ref[0:dirs, 0:1] * off_ref[0]
        + table_ref[0:dirs, 1:2] * off_ref[1]
        + table_ref[0:dirs, 2:3] * off_ref[2]
    )
    cos_s = jnp.cos(phases)
    sin_s = jnp.sin(phases)
    cos_b = table_ref[dirs : dirs + boxes, :]
    sin_b = table_ref[dirs + boxes : dirs + 2 * boxes, :]
    member = (iota((boxes, spheres), 0) == box_ref[...]).astype(F32).astype(BF16)
    member_t = (iota((LANES, spheres), 0) == box_ref[...]).astype(F32).T[:, :boxes].astype(BF16)
    for c in range(2):
        send_pat[c * dirs : (c + 1) * dirs, :] = pat_ref[c].astype(F32).T.astype(BF16)

    z_rows = [(-1, 0), (1, 0)]
    y_rows = [(0, -1), (0, 1)]
    corners = [(-1, -1), (-1, 1), (1, -1), (1, 1)]
    row_args = (row_block, rows_send, rows_recv)
    leaf_args = (leaf_block, leafs_send, leafs_recv)

    def outgoing(it):
        own_rows = rows[it, :, mid * spheres : (mid + 1) * spheres]
        wide = jnp.concatenate([own_rows[:coefs], own_rows[coefs:]], axis=1)
        sig = dot_nn(send_pat[...], wide)
        sig_r = sig[:dirs, :spheres] - sig[dirs:, spheres:]
        sig_i = sig[dirs:, :spheres] + sig[:dirs, spheres:]
        out = jnp.concatenate(
            [sig_r * cos_s + sig_i * sin_s, sig_i * cos_s - sig_r * sin_s], axis=0
        )
        high = out.astype(BF16)
        low = (out - high.astype(F32)).astype(BF16)
        leaf_t = dot_nt(member, high) + dot_nt(member, low)
        leafs[it, own * boxes : (own + 1) * boxes, :] = leaf_t.astype(BF16)
        lr, li = leaf_t[:, :dirs], leaf_t[:, dirs:]
        up_r = jnp.sum(lr * cos_b + li * sin_b, axis=0, keepdims=True)
        up_i = jnp.sum(li * cos_b - lr * sin_b, axis=0, keepdims=True)
        colsrc[it] = jnp.concatenate([up_r, up_i], axis=0)

    def send_rest(it):
        send_all(colsrc.at[it], cols.at[it], cols_send.at[it], cols_recv.at[it])
        send_to(around, *leaf_args, it)
        send_to(corners, *row_args, it)
        send_to(y_rows, *row_args, it)

    outgoing(0)
    pl.semaphore_wait(barrier, n - 1)
    send_to(z_rows, *row_args, 0)
    send_rest(0)

    for it in range(2):
        for dx, dy in around:
            @pl.when(jnp.logical_not(inside(dx, dy)))
            def _():
                s = slot(dx, dy)
                p = places[s]
                rows[it, :, p * spheres : (p + 1) * spheres] = jnp.zeros((coefs2, spheres), BF16)
                leafs[it, s * boxes : (s + 1) * boxes, :] = jnp.zeros((boxes, 2 * dirs), BF16)

    cosT[...] = cos_s.T
    sinT[...] = sin_s.T
    ready("mie", "rec", "leaf", "fsrc", "fcls", "src", "dst")
    for c in range(2):
        mief[c] = jnp.dot(
            table_ref[0:coefs, 8 : 8 + mies],
            mie_ref[c * mies : (c + 1) * mies, :],
            precision=HIGHEST,
            preferred_element_type=F32,
        )
    take_r, take_i = rec_ref[0], rec_ref[1]
    take[...] = jnp.concatenate(
        [jnp.concatenate([take_r, -take_i], axis=1), jnp.concatenate([take_i, take_r], axis=1)],
        axis=0,
    )
    entries = boxes * list_len

    def entry_box(shape, dim):
        place = iota(shape, dim).astype(F32)
        return place, jnp.floor((place + 0.5) * (1.0 / list_len))

    place, its_box = entry_box((entries, boxes), 0)
    box_hot = (its_box == iota((entries, boxes), 1).astype(F32)).astype(F32)
    place, its_box = entry_box((entries, list_len), 0)
    list_hot = (place - list_len * its_box == iota((entries, list_len), 1).astype(F32)).astype(F32)

    def flat(ref):
        spread = jnp.dot(
            box_hot, ref[...].astype(F32), precision=HIGHEST, preferred_element_type=F32
        )
        return jnp.sum(spread * list_hot, axis=1, keepdims=True)

    nine = 9 * boxes
    pickhot[...] = (
        (flat(fsrc_ref) == iota((entries, nine), 1).astype(F32)).astype(F32).astype(BF16)
    )
    class_hot = (flat(fcls_ref) == iota((entries, leaf_classes), 1).astype(F32)).astype(F32)
    for c in range(2):
        chosen[c] = jnp.dot(
            class_hot, leaf_ref[:, c, :], precision=HIGHEST, preferred_element_type=F32
        )

    def count(pair, carry):
        here = iota((spheres, pairs), 0)
        for part in range(2):
            k = 2 * pair + part
            src = src_ref[pl.ds(k, 1), :]
            source = jnp.concatenate(
                [(here == src - slot(*o) * spheres).astype(F32).astype(BF16) for o in order], axis=0
            )
            target = (here == dst_ref[pl.ds(k, 1), :]).astype(F32).astype(BF16)
            counts[pair, :, part * spheres : (part + 1) * spheres] = dot_nt(source, target).astype(
                BF16
            )
        return carry

    lax.fori_loop(0, classes // 2, count, 0)
    ready("near", "coarse")
    tcat[...] = jnp.zeros(tcat.shape, BF16)
    gcat[...] = jnp.zeros(gcat.shape, BF16)
    for k in range(classes):
        tcat[:, k * LANES : k * LANES + coefs] = near_ref[k]

    def near_group(it, first, last, start):
        low, high = first * spheres, last * spheres

        def near_pair(pair, carry):
            gathered = dot_nn(rows[it, :, low:high], counts[pair, low:high, :]).astype(BF16)
            for part in range(2):
                one = gathered[:, part * spheres : (part + 1) * spheres]
                wide = jnp.concatenate([one[:coefs], one[coefs:]], axis=1)
                base = pl.multiple_of((2 * pair + part) * LANES, LANES)
                gcat[pl.ds(base, coefs), :] = wide
            return carry

        lax.fori_loop(0, classes // 2, near_pair, 0, unroll=2)
        total = dot_nn(tcat[...], gcat[...])
        near_acc[...] = total if start else near_acc[...] + total

    def incoming_field(it):
        wait_from(y_rows, *row_args, it)
        wait_from(z_rows, *row_args, it)
        near_group(it, 0, 5, True)

        wait_from(around, *leaf_args, it)
        picked = dot_nn(pickhot[...], leafs[it])
        pr, pi = picked[:, :dirs], picked[:, dirs:]
        cr, ci = chosen[0], chosen[1]
        leaf_r = jnp.sum((pr * cr - pi * ci).reshape(boxes, list_len, dirs), axis=1)
        leaf_i = jnp.sum((pr * ci + pi * cr).reshape(boxes, list_len, dirs), axis=1)

        wait_bytes(cols.at[it], cols_recv.at[it])
        cols[it, me] = colsrc[it]

        def column(x, acc):
            straight, crossed = acc
            apart_y = jnp.abs(lax.broadcasted_iota(jnp.int32, (n_y, 2, dirs), 0) - py)
            away = jnp.maximum(apart_y, jnp.abs(x - px)) >= 2
            value = jnp.where(away, cols[it, pl.ds(x * n_y, n_y)], 0.0)
            w = coarse_ref[x + (n_x - 1) - px, pl.ds((n_y - 1) - py, n_y)]
            return (
                straight + jnp.sum(value * w[:, 0:1], axis=0),
                crossed + jnp.sum(value * w[:, 1:2], axis=0),
            )

        zero = jnp.zeros((2, dirs), F32)
        straight, crossed = lax.fori_loop(
            0, n_x, column, (zero, zero), unroll=4 if n_x % 4 == 0 else 1
        )
        col_r = straight[0:1] - crossed[1:2]
        col_i = straight[1:2] + crossed[0:1]
        in_r = leaf_r + (col_r * cos_b - col_i * sin_b)
        in_i = leaf_i + (col_r * sin_b + col_i * cos_b)
        both = jnp.concatenate([in_r, in_i], axis=1)
        high = both.astype(BF16)
        low = (both - high.astype(F32)).astype(BF16)
        spread = dot_nn(member_t, high) + dot_nn(member_t, low)
        sr, si = spread[:, :dirs], spread[:, dirs:]
        ct, st = cosT[...], sinT[...]
        arriving = jnp.concatenate([sr * ct - si * st, sr * st + si * ct], axis=1).astype(BF16)
        far = dot_nt(take[...], arriving)
        wait_from(corners, *row_args, it)
        near_group(it, 5, 9, False)
        near = near_acc[...]
        near_r = near[:coefs, :spheres] - near[coefs:, spheres:]
        near_i = near[coefs:, :spheres] + near[:coefs, spheres:]
        fr = near_r + far[:coefs]
        fi = near_i + far[coefs:]
        mr, mi = mief[0], mief[1]
        return jnp.concatenate([fr * mr - fi * mi, fr * mi + fi * mr], axis=0)

    y = incoming_field(0)
    y_ref[...] = y
    rows[1, :, mid * spheres : (mid + 1) * spheres] = y.astype(BF16)
    send_to(z_rows, *row_args, 1)
    outgoing(1)
    send_rest(1)
    v = inc_ref[...]
    y = y_ref[...]

    def total(a, b):
        return jnp.sum(jnp.sum(a * b, axis=0, keepdims=True), axis=1, keepdims=True)

    g00, g01, g11 = total(v, v), total(v, y), total(y, y)
    z = incoming_field(1)
    v = inc_ref[...]
    y = y_ref[...]
    lane = iota((1, LANES), 1)
    row = jnp.zeros((1, LANES), F32)
    for i, value in enumerate((g00, g01, g11, total(v, z), total(y, z), total(z, z))):
        row = jnp.where(lane == i, value, row)
    sumsrc[...] = row
    send_all(sumsrc, sums, sums_send, sums_recv)
    for it in range(2):
        wait_sent(*row_args, it)
        wait_sent(*leaf_args, it)
        wait_bytes(cols.at[it], cols_send.at[it])
    wait_bytes(sums, sums_send)
    wait_bytes(sums, sums_recv)
    sums[me] = row
    totals = jnp.sum(sums[...], axis=0)
    s00, s01, s11, s02, s12, s22 = (
        jnp.sum(jnp.where(lane == i, totals, 0.0), axis=1, keepdims=True) for i in range(6)
    )
    beta = jnp.sqrt(s00)
    a = s01 / s00
    h10 = jnp.sqrt((s11 - a * s01) / s00)
    g = 1.0 / (beta * h10)
    h00 = 1.0 - a
    d = (g / beta) * (a * s01 - s02)
    c = g * g * (a * (a * s01 - s02 - s11) + s12)
    e = g * g * (a * (a * s11 - 2.0 * s12) + s22)
    h21 = jnp.sqrt(e - c * c - d * d)
    h01 = -d
    h11 = 1.0 - c
    n11 = h00 * h00 + h10 * h10
    n12 = h00 * h01 + h10 * h11
    n22 = h01 * h01 + h11 * h11 + h21 * h21
    l11 = jnp.sqrt(n11)
    l21 = n12 / l11
    l22 = jnp.sqrt(n22 - l21 * l21)
    m0 = beta * h00 / l11
    m1 = (beta * h01 - l21 * m0) / l22
    w1 = m1 / l22
    w0 = (m0 - l21 * w1) / l11
    f0 = h00 * w0 + h01 * w1
    f1 = h10 * w0 + h11 * w1
    ga = g * a
    sol_ref[...] = (w0 / beta + w1 * ga) * v - (w1 * g) * y
    res_ref[...] = (
        ((beta - f0) / beta - f1 * ga - w1 * (d / beta + c * ga)) * v
        + (f1 * g + w1 * (ga + c * g)) * y
        - (w1 * g) * z
    )


def local(n_x, n_y, *args):
    (
        incident,
        mie,
        offsets,
        sphere_box,
        near_table,
        near_src,
        near_dst,
        pattern,
        receive,
        leaf_transfer,
        far_src,
        far_cls,
        coarse_transfer,
    ) = args
    coefs = incident.shape[1]
    spheres = incident.shape[4]
    mies = mie.shape[1]
    dirs = pattern.shape[1]
    pat_t = pattern.transpose(0, 2, 1)
    coarse_t = coarse_transfer.transpose(1, 2, 0, 3)
    boxes, list_len = far_src.shape[2:]
    classes, pairs = near_src.shape[2:]
    n = n_x * n_y
    coefs2 = 2 * coefs
    entries = boxes * list_len
    table = jnp.asarray(constants(dirs, boxes, coefs, mies))
    operands = (
        table,
        incident.reshape(coefs2, spheres),
        mie.reshape(2 * mies, spheres),
        offsets.reshape(3, 1, spheres),
        sphere_box.reshape(1, spheres),
        near_table.reshape(classes, coefs2, coefs),
        near_src.reshape(classes, pairs),
        near_dst.reshape(classes, pairs),
        pat_t,
        receive,
        leaf_transfer,
        far_src.reshape(boxes, list_len),
        far_cls.reshape(boxes, list_len),
        coarse_t,
    )
    vmem = pl.BlockSpec(memory_space=pltpu.VMEM)
    shape = jax.ShapeDtypeStruct((coefs2, spheres), F32)
    dma = pltpu.SemaphoreType.DMA
    sol, res = pl.pallas_call(
        functools.partial(kernel, n_x, n_y),
        out_shape=(shape, shape),
        in_specs=[pl.BlockSpec(memory_space=pltpu.HBM)] * len(operands),
        out_specs=(vmem, vmem),
        scratch_shapes=[pltpu.VMEM(x.shape, x.dtype) for x in operands]
        + [
            dma((len(operands),)),
            pltpu.VMEM((2, coefs2, 9 * spheres), BF16),
            pltpu.VMEM((2, 9 * boxes, 2 * dirs), BF16),
            pltpu.VMEM((2, n, 2, dirs), F32),
            pltpu.VMEM((2, 2, dirs), F32),
            pltpu.VMEM((n, 1, LANES), F32),
            pltpu.VMEM((1, LANES), F32),
            pltpu.VMEM((classes // 2, 9 * spheres, 2 * spheres), BF16),
            pltpu.VMEM((coefs2, spheres), F32),
            pltpu.VMEM((2, coefs, spheres), F32),
            pltpu.VMEM((spheres, dirs), F32),
            pltpu.VMEM((spheres, dirs), F32),
            pltpu.VMEM((2, entries, dirs), F32),
            pltpu.VMEM((entries, 9 * boxes), BF16),
            pltpu.VMEM((coefs2, 2 * dirs), BF16),
            pltpu.VMEM((2 * dirs, coefs), BF16),
            pltpu.VMEM((coefs2, classes * LANES), BF16),
            pltpu.VMEM((classes * LANES, 2 * spheres), BF16),
            pltpu.VMEM((coefs2, 2 * spheres), F32),
            dma((2, 9)),
            dma((2, 9)),
            dma((2, 9)),
            dma((2, 9)),
            dma((2,)),
            dma((2,)),
            dma,
            dma,
        ],
        compiler_params=pltpu.CompilerParams(
            collective_id=0, has_side_effects=True, vmem_limit_bytes=60 * 1024 * 1024
        ),
    )(*operands)
    return sol.reshape(incident.shape), res.reshape(incident.shape)


def solution(mesh):
    field = P(None, None, "bx", "by", None)
    placed = (
        field,
        field,
        P(None, "bx", "by", None),
        P("bx", "by", None),
        P(),
        P("bx", "by", None, None),
        P("bx", "by", None, None),
        P(),
        P(),
        P(),
        P("bx", "by", None, None),
        P("bx", "by", None, None),
        P(),
    )
    return jax.shard_map(
        functools.partial(local, mesh.shape["bx"], mesh.shape["by"]),
        mesh=mesh,
        in_specs=placed,
        out_specs=(field, field),
        check_vma=False,
    )
```
